128 devices in a mesh: wide: 32 (over x, y, z_hi), narrow: 4 (over z_lo, core).
Axes of the slice: x: 4, y: 4, z: 4 (z_hi: 2, z_lo: 2; z = z_hi * 2 + z_lo), core: 2. Of those that a mesh axis runs over, the one named last changes fastest.
Arguments:
- coefficients: float32 [8, 8192, 8192], P(None, 'wide', 'narrow'), may hold values from -0.07 to 0.07
- tensor_blocks: float32 [8, 32, 8192], P(None, 'wide', 'narrow'), may hold values from -6 to 6
- basis_rows: float32 [32, 8192], P(None, ('wide', 'narrow')), may hold values from -1.1 to 1.1, as said below
Outputs:
- new_basis: float32 [32, 8192], P(None, ('wide', 'narrow'))
- projection: float32 [32, 32], replicated
- factor: float32 [32, 32], replicated
The draws below stay inside these ranges and needn't reach their ends.
Inputs may be any that keep to these rules, and one draw needn't show every extreme that they name: The rows of basis_rows are nearly but not exactly orthonormal: basis_rows basis_rows^T differs from the identity by less than 0.2 in spectral norm.
All inputs are finite; a program needn't handle non-finite values.
Results may differ from the reference program's by a relative error of at most 0.0002.
Values sent between devices are 32-bit elements; how exact they have to be, the bound alone decides.
No kernel may reach another device: no remote copies, remote signals or barrier semaphores. Data moves between devices by JAX's collectives and lax.ppermute only.
A program may use at most 64 MiB of HBM per device.

```python
import math
import jax
import jax.numpy as jnp
from jax import lax

N = 8192
K = 8
R = 32
M = 32


def orthonormal_rows(raw):
    hi = lax.Precision.HIGHEST
    for sweep in range(2):
        gram = jnp.dot(raw, raw.T, precision=hi)
        lower = jnp.linalg.cholesky(gram)
        raw = lax.linalg.triangular_solve(lower, raw, left_side=True, lower=True)
    return raw


def coefficient_values(key):
    spread = 0.5 / math.sqrt(K * N)
    inner_key = jax.random.fold_in(key, 11)
    values = jnp.clip(jax.random.normal(inner_key, (K, N, N), jnp.float32), -6.0, 6.0) * spread
    return values


def tensor_values(key):
    inner_key = jax.random.fold_in(key, 12)
    values = jnp.clip(jax.random.normal(inner_key, (K, R, N), jnp.float32), -6.0, 6.0)
    return values


def draw_coefficients(key, part):
    return coefficient_values(key).astype(jnp.float32)


def draw_tensor_blocks(key, part):
    return tensor_values(key).astype(jnp.float32)


def draw_basis_rows(key, part):
    hi = lax.Precision.HIGHEST
    image = jnp.einsum('kic,krc->ir', tensor_values(key), coefficient_values(key), precision=hi)
    noise_key = jax.random.fold_in(key, 13)
    turn_key = jax.random.fold_in(key, 14)
    noise = jax.random.normal(noise_key, (M, N), jnp.float32)
    tilt = 0.06
    frame = orthonormal_rows(image[:M] + 0.1 * noise)
    turn = orthonormal_rows(jax.random.normal(turn_key, (M, M), jnp.float32))
    mixer = jnp.eye(M, dtype=jnp.float32) + tilt * turn
    return jnp.dot(mixer, frame, precision=hi).astype(jnp.float32)


def setup_inputs(seed: int = 0) -> dict:
    seeds = jax.random.split(jax.random.key(seed), 4)
    return {
        "coefficients": draw_coefficients(jax.random.fold_in(seeds[3], 71), 0),
        "tensor_blocks": draw_tensor_blocks(jax.random.fold_in(seeds[3], 71), 0),
        "basis_rows": draw_basis_rows(jax.random.fold_in(seeds[3], 71), 0),
    }


def reference(coefficients, tensor_blocks, basis_rows):
    hi = lax.Precision.HIGHEST
    image = jnp.einsum('kic,krc->ir', tensor_blocks, coefficients, precision=hi)
    first = jnp.dot(basis_rows, image.T, precision=hi)
    once = image - jnp.dot(first.T, basis_rows, precision=hi)
    second = jnp.dot(basis_rows, once.T, precision=hi)
    twice = once - jnp.dot(second.T, basis_rows, precision=hi)
    gram = jnp.dot(twice, twice.T, precision=hi) / N
    factor = jnp.linalg.cholesky(gram)
    new_basis = lax.linalg.triangular_solve(factor, twice, left_side=True, lower=True)
    return (new_basis, first + second, factor)
```

```python
import functools

import jax
import jax.numpy as jnp
from jax import lax
from jax.experimental import pallas as pl
from jax.experimental.pallas import tpu as pltpu
from jax.sharding import PartitionSpec as P

N = 8192
K = 8
R = 32
XS = 4
YS = 4
HALF = 1024
AXES = ("wide", "narrow")
HI = lax.Precision.HIGHEST
NT = (((1,), (1,)), ((), ()))
NN = (((1,), (0,)), ((), ()))
VM = pl.BlockSpec(memory_space=pltpu.VMEM)


def flat(x, y, zh, zl, core):
    return ((x * YS + y) * 2 + zh) * 4 + zl * 2 + core


def sources(source_of):
    pairs = []
    for x in range(XS):
        for y in range(YS):
            for zh in range(2):
                for zl in range(2):
                    for core in range(2):
                        here = (x, y, zh, zl, core)
                        pairs.append((flat(*source_of(*here)), flat(*here)))
    return pairs


def from_x(step):
    return sources(lambda x, y, zh, zl, core: ((x + step) % XS, y, zh, zl, core))


def from_y(step):
    return sources(lambda x, y, zh, zl, core: (x, (y + step) % YS, zh, zl, core))


FROM_ZH = sources(lambda x, y, zh, zl, core: (x, y, 1 - zh, zl, core))
FROM_ZL = sources(lambda x, y, zh, zl, core: (x, y, zh, 1 - zl, core))
FROM_CORE = sources(lambda x, y, zh, zl, core: (x, y, zh, zl, 1 - core))
FROM_Z = sources(lambda x, y, zh, zl, core: (x, y, 1 - zh, 1 - zl, core))
EVEN = (1, 0, 3, 2)
ODD = (3, 2, 1, 0)


def pair_x(partner):
    return sources(lambda x, y, zh, zl, core: (partner[x], y, zh, zl, core))


def pair_y(partner):
    return sources(lambda x, y, zh, zl, core: (x, partner[y], zh, zl, core))


def move(value, pairs):
    return lax.ppermute(value, AXES, pairs)


def split(value):
    high = value.astype(jnp.bfloat16)
    low = (value - high.astype(jnp.float32)).astype(jnp.bfloat16)
    return high, low


def split_kernel(block_ref, high_ref, low_ref):
    k = pl.program_id(0)
    high, low = split(block_ref[0])
    high_ref[k] = high
    low_ref[k] = low


def split_coefficients(coefficients):
    shape = coefficients.shape
    out = pltpu.VMEM(shape, jnp.bfloat16)
    return pl.pallas_call(
        split_kernel,
        grid=(shape[0],),
        in_specs=[pl.BlockSpec((1, *shape[1:]), lambda k: (k, 0, 0))],
        out_specs=[VM, VM],
        out_shape=[out, out],
        compiler_params=pltpu.CompilerParams(vmem_limit_bytes=10 << 20),
        name="split",
    )(coefficients)


def image_kernel(place_ref, *refs):
    pieces = (refs[0:4], refs[4:8])
    high_ref, low_ref, out_ref, held = refs[8:]
    for half in range(2):
        total = None
        for k in range(K):
            rows = jnp.concatenate([piece[:, k, :] for piece in pieces[half]], axis=0)
            rows_high, rows_low = split(rows)
            both = jnp.concatenate([rows_high, rows_low], axis=0)
            cols = pl.ds(half * HALF, HALF)
            main = lax.dot_general(both, high_ref[k, :, cols], NT, preferred_element_type=jnp.float32)
            rest = lax.dot_general(rows_high, low_ref[k, :, cols], NT, preferred_element_type=jnp.float32)
            part = main[:R] + main[R:] + rest
            total = part if total is None else total + part
        held[half] = total
    x0, y0, zh0 = place_ref[0], place_ref[1], place_ref[2]
    for x in range(XS):
        for y in range(YS):
            for zh in range(2):
                dx = (x - x0 + XS) % XS
                dy = (y - y0 + YS) % YS
                dz = (zh + zh0) % 2
                a = held[0, pl.ds(dy * 8 + dx * 2 + dz, 1), :]
                b = held[1, pl.ds(dx * 8 + dy * 2 + dz, 1), :]
                out_ref[pl.ds((x * YS + y) * 2 + zh, 1), :] = a + b


def image_part(place, pieces, high, low):
    rows = high.shape[1]
    return pl.pallas_call(
        image_kernel,
        in_specs=[pl.BlockSpec(memory_space=pltpu.SMEM)] + [VM] * 10,
        out_specs=VM,
        out_shape=jax.ShapeDtypeStruct((R, rows), jnp.float32),
        scratch_shapes=[pltpu.VMEM((2, R, rows), jnp.float32)],
        compiler_params=pltpu.CompilerParams(vmem_limit_bytes=6 << 20),
        name="image",
    )(place, *pieces, high, low)


def products_kernel(mine_ref, other_ref, basis_ref, image_ref, products_ref):
    image = mine_ref[...] + other_ref[...]
    image_ref[...] = image
    basis = basis_ref[...]
    both = jnp.concatenate([image, basis], axis=0)
    of_image = lax.dot_general(image, both, NT, precision=HI, preferred_element_type=jnp.float32)
    of_basis = lax.dot_general(basis, both, NT, precision=HI, preferred_element_type=jnp.float32)
    products_ref[...] = jnp.concatenate([of_image, of_basis], axis=1)


def products(mine, other, basis):
    return pl.pallas_call(
        products_kernel,
        in_specs=[VM] * 3,
        out_specs=[VM] * 2,
        out_shape=[
            jax.ShapeDtypeStruct(mine.shape, jnp.float32),
            jax.ShapeDtypeStruct((R, 4 * R), jnp.float32),
        ],
        compiler_params=pltpu.CompilerParams(vmem_limit_bytes=2 << 20),
        name="products",
    )(mine, other, basis)


def final_kernel(place_ref, products_ref, image_ref, basis_ref, new_ref, projection_ref, factor_ref):
    dot = functools.partial(lax.dot_general, precision=HI, preferred_element_type=jnp.float32)
    squares = products_ref[:, 0:R]
    first_t = products_ref[:, R : 2 * R]
    first = products_ref[:, 2 * R : 3 * R]
    basis_gram = products_ref[:, 3 * R : 4 * R]
    projection = 2.0 * first - dot(basis_gram, first, NN)
    projection_t = 2.0 * first_t - dot(first_t, basis_gram, NN)
    projection_ref[...] = projection
    left = first - dot(basis_gram, projection, NN)
    gram = (squares - dot(first_t, projection, NN) - dot(projection_t, left, NN)) / N
    narrow = place_ref[3]
    own = image_ref[:, 0:64]
    for n in range(1, 4):
        own = jnp.where(narrow == n, image_ref[:, n * 64 : (n + 1) * 64], own)
    twice = own - dot(projection_t, basis_ref[...], NN)
    work = jnp.concatenate([gram, jnp.zeros((R, R), jnp.float32), twice], axis=1)
    lane = lax.broadcasted_iota(jnp.int32, (1, 4 * R), 1)
    done = []
    for k in range(R):
        row = work[k : k + 1, :]
        column = work[:, k : k + 1]
        scale = 1.0 / jnp.sqrt(work[k : k + 1, k : k + 1])
        unit = row * scale
        done.append(jnp.where(lane >= k, unit, 0.0))
        work = work - (column * scale) * unit
    rows = jnp.concatenate(done, axis=0)
    factor_ref[...] = rows[:, 0:R].T
    new_ref[...] = rows[:, 2 * R : 4 * R]


def final(place, total, image, basis):
    return pl.pallas_call(
        final_kernel,
        in_specs=[pl.BlockSpec(memory_space=pltpu.SMEM)] + [VM] * 3,
        out_specs=[VM] * 3,
        out_shape=[
            jax.ShapeDtypeStruct(basis.shape, jnp.float32),
            jax.ShapeDtypeStruct((R, R), jnp.float32),
            jax.ShapeDtypeStruct((R, R), jnp.float32),
        ],
        compiler_params=pltpu.CompilerParams(vmem_limit_bytes=2 << 20),
        name="final",
    )(place, total, image, basis)


def body(coefficients, tensor_blocks, basis_rows):
    wide = lax.axis_index("wide")
    narrow = lax.axis_index("narrow")
    place = jnp.stack([wide // (2 * YS), (wide // 2) % YS, wide % 2, narrow]).astype(jnp.int32)

    own = tensor_blocks.reshape(K, 2 * HALF)
    across = move(own, FROM_ZH)
    pair = jnp.stack([own, across])
    a, b = pair[:, :, :HALF], pair[:, :, HALF:]
    a = jnp.concatenate([a] + [move(a, from_x(s)) for s in (1, 2, 3)])
    b = jnp.concatenate([b] + [move(b, from_y(s)) for s in (1, 2, 3)])
    pieces_a = [a] + [move(a, from_y(s)) for s in (1, 2, 3)]
    pieces_b = [b] + [move(b, from_x(s)) for s in (1, 2, 3)]

    high, low = split_coefficients(coefficients)

    other = move(basis_rows, FROM_CORE)
    at_core = narrow % 2 == 0
    basis = jnp.concatenate([jnp.where(at_core, basis_rows, other), jnp.where(at_core, other, basis_rows)], axis=1)
    other = move(basis, FROM_ZL)
    at_zl = narrow // 2 == 0
    basis = jnp.concatenate([jnp.where(at_zl, basis, other), jnp.where(at_zl, other, basis)], axis=1)

    part = image_part(place, pieces_a + pieces_b, high, low)
    part = part + move(part, FROM_CORE)
    image, total = products(part, move(part, FROM_ZL), basis)
    for pairs in (FROM_Z, pair_x(EVEN), pair_x(ODD), pair_y(EVEN), pair_y(ODD)):
        total = total + move(total, pairs)
    return tuple(final(place, total, image, basis_rows))


def solution(mesh):
    in_specs = (P(None, "wide", "narrow"), P(None, "wide", "narrow"), P(None, ("wide", "narrow")))
    out_specs = (P(None, ("wide", "narrow")), P(), P())
    return jax.shard_map(body, mesh=mesh, in_specs=in_specs, out_specs=out_specs, check_vma=False)
```

```python
import functools

import jax
import jax.numpy as jnp
from jax import lax
from jax.experimental import pallas as pl
from jax.experimental.pallas import tpu as pltpu
from jax.sharding import Mesh, PartitionSpec as P

N = 8192
K = 8
R = 32
XS = 4
YS = 4
HALF = 1024
ROWS = 256
OWN = 64
AXES = ("x", "y", "zh", "zl", "core")
HI = lax.Precision.HIGHEST
NT = (((1,), (1,)), ((), ()))
NN = (((1,), (0,)), ((), ()))
VM = pl.BlockSpec(memory_space=pltpu.VMEM)
SM = pl.BlockSpec(memory_space=pltpu.SMEM)


def flat(x, y, zh, zl, core):
    return ((x * YS + y) * 2 + zh) * 4 + zl * 2 + core


def sources(source_of):
    pairs = []
    for x in range(XS):
        for y in range(YS):
            for zh in range(2):
                for zl in range(2):
                    for core in range(2):
                        here = (x, y, zh, zl, core)
                        pairs.append((flat(*source_of(*here)), flat(*here)))
    return pairs


def from_x(step):
    return sources(lambda x, y, zh, zl, core: ((x + step) % XS, y, zh, zl, core))


def from_y(step):
    return sources(lambda x, y, zh, zl, core: (x, (y + step) % YS, zh, zl, core))


FROM_ZH = sources(lambda x, y, zh, zl, core: (x, y, 1 - zh, zl, core))
FROM_CORE = sources(lambda x, y, zh, zl, core: (x, y, zh, zl, 1 - core))
FROM_ZL = sources(lambda x, y, zh, zl, core: (x, y, zh, 1 - zl, 1 - core))
FROM_Z = sources(lambda x, y, zh, zl, core: (x, y, 1 - zh, 1 - zl, 1 - core))


def move(value, pairs):
    return lax.ppermute(value, AXES, pairs)


def split(value):
    high = value.astype(jnp.bfloat16)
    low = (value - high.astype(jnp.float32)).astype(jnp.bfloat16)
    return high, low


def load_kernel(source_ref, out_ref, sem):
    copy = pltpu.make_async_copy(source_ref, out_ref, sem)
    copy.start()
    copy.wait()


def load(coefficients):
    return pl.pallas_call(
        load_kernel,
        in_specs=[pl.BlockSpec(memory_space=pltpu.HBM)],
        out_specs=VM,
        out_shape=pltpu.VMEM(coefficients.shape, jnp.float32),
        scratch_shapes=[pltpu.SemaphoreType.DMA],
        compiler_params=pltpu.CompilerParams(vmem_limit_bytes=1 << 20),
        name="load",
    )(coefficients)


def half_image(half, place_ref, pieces, block, held):
    total = None
    for k in range(K):
        rows = jnp.concatenate([piece[:, k, :] for piece in pieces], axis=0)
        rows_high, rows_low = split(rows)
        both = jnp.concatenate([rows_high, rows_low], axis=0)
        high, low = split(block[k, :, half * HALF : (half + 1) * HALF])
        main = lax.dot_general(both, high, NT, preferred_element_type=jnp.float32)
        rest = lax.dot_general(rows_high, low, NT, preferred_element_type=jnp.float32)
        part = main[:R] + main[R:] + rest
        total = part if total is None else total + part
    held[...] = total
    x0, y0, zh0 = place_ref[0], place_ref[1], place_ref[2]
    ordered = []
    for x in range(XS):
        for y in range(YS):
            for zh in range(2):
                dx = (x - x0 + XS) % XS
                dy = (y - y0 + YS) % YS
                dz = (zh + zh0) % 2
                outer, inner = (dy, dx) if half == 0 else (dx, dy)
                ordered.append(held[pl.ds(outer * 8 + inner * 2 + dz, 1), :])
    return ordered


def first_half_kernel(place_ref, *refs):
    pieces, (block, out_ref, held) = refs[:4], refs[4:]
    for i, row in enumerate(half_image(0, place_ref, pieces, block, held)):
        out_ref[i : i + 1, :] = row


def second_half_kernel(place_ref, *refs):
    pieces, (block, first_ref, basis_ref, out_ref, held) = refs[:4], refs[4:]
    for i, row in enumerate(half_image(1, place_ref, pieces, block, held)):
        out_ref[i : i + 1, 0:ROWS] = first_ref[i : i + 1, :] + row
    out_ref[:, ROWS : ROWS + OWN] = basis_ref[...]
    out_ref[:, ROWS + OWN :] = jnp.zeros_like(basis_ref)


def image_call(kernel, name, width, *args):
    return pl.pallas_call(
        kernel,
        in_specs=[SM] + [VM] * (len(args) - 1),
        out_specs=VM,
        out_shape=jax.ShapeDtypeStruct((R, width), jnp.float32),
        scratch_shapes=[pltpu.VMEM((R, ROWS), jnp.float32)],
        compiler_params=pltpu.CompilerParams(vmem_limit_bytes=6 << 20),
        name=name,
    )(*args)


def in_order(second, mine, other):
    return jnp.concatenate([jnp.where(second, other, mine), jnp.where(second, mine, other)], axis=1)


def pair_kernel(place_ref, mine_ref, other_ref, out_ref):
    out_ref[:, 0:ROWS] = mine_ref[:, 0:ROWS] + other_ref[:, 0:ROWS]
    own = slice(ROWS, ROWS + OWN)
    out_ref[:, ROWS:] = in_order(place_ref[4] == 1, mine_ref[:, own], other_ref[:, own])


def pair(place, mine, other):
    return pl.pallas_call(
        pair_kernel,
        in_specs=[SM, VM, VM],
        out_specs=VM,
        out_shape=jax.ShapeDtypeStruct(mine.shape, jnp.float32),
        compiler_params=pltpu.CompilerParams(vmem_limit_bytes=2 << 20),
        name="pair",
    )(place, mine, other)


def products_kernel(place_ref, mine_ref, other_ref, image_ref, products_ref):
    image = mine_ref[:, 0:ROWS] + other_ref[:, 0:ROWS]
    image_ref[...] = image
    basis = in_order(place_ref[3] == 1, mine_ref[:, ROWS:], other_ref[:, ROWS:])
    both = jnp.concatenate([image, basis], axis=0)
    of_image = lax.dot_general(image, both, NT, precision=HI, preferred_element_type=jnp.float32)
    of_basis = lax.dot_general(basis, both, NT, precision=HI, preferred_element_type=jnp.float32)
    products_ref[...] = jnp.concatenate([of_image, of_basis], axis=1)


def products(place, mine, other):
    return pl.pallas_call(
        products_kernel,
        in_specs=[SM, VM, VM],
        out_specs=[VM] * 2,
        out_shape=[
            jax.ShapeDtypeStruct((R, ROWS), jnp.float32),
            jax.ShapeDtypeStruct((R, 4 * R), jnp.float32),
        ],
        compiler_params=pltpu.CompilerParams(vmem_limit_bytes=2 << 20),
        name="products",
    )(place, mine, other)


def final_kernel(place_ref, products_ref, image_ref, basis_ref, new_ref, projection_ref, factor_ref):
    dot = functools.partial(lax.dot_general, precision=HI, preferred_element_type=jnp.float32)
    total = products_ref[0]
    for chip in range(1, XS * YS):
        total = total + products_ref[chip]
    squares = total[:, 0:R]
    first_t = total[:, R : 2 * R]
    first = total[:, 2 * R : 3 * R]
    basis_gram = total[:, 3 * R : 4 * R]
    projection = 2.0 * first - dot(basis_gram, first, NN)
    projection_t = 2.0 * first_t - dot(first_t, basis_gram, NN)
    projection_ref[...] = projection
    left = first - dot(basis_gram, projection, NN)
    gram = (squares - dot(first_t, projection, NN) - dot(projection_t, left, NN)) / N
    narrow = place_ref[3] * 2 + place_ref[4]
    own = image_ref[:, 0:64]
    for n in range(1, 4):
        own = jnp.where(narrow == n, image_ref[:, n * 64 : (n + 1) * 64], own)
    twice = own - dot(projection_t, basis_ref[...], NN)
    work = jnp.concatenate([gram, jnp.zeros((R, R), jnp.float32), twice], axis=1)
    lane = lax.broadcasted_iota(jnp.int32, (1, 4 * R), 1)
    done = []
    for k in range(R):
        row = work[k : k + 1, :]
        column = work[:, k : k + 1]
        scale = 1.0 / jnp.sqrt(work[k : k + 1, k : k + 1])
        unit = row * scale
        done.append(jnp.where(lane >= k, unit, 0.0))
        work = work - (column * scale) * unit
    rows = jnp.concatenate(done, axis=0)
    factor_ref[...] = rows[:, 0:R].T
    new_ref[...] = rows[:, 2 * R : 4 * R]


def final(place, total, image, basis):
    return pl.pallas_call(
        final_kernel,
        in_specs=[SM] + [VM] * 3,
        out_specs=[VM] * 3,
        out_shape=[
            jax.ShapeDtypeStruct(basis.shape, jnp.float32),
            jax.ShapeDtypeStruct((R, R), jnp.float32),
            jax.ShapeDtypeStruct((R, R), jnp.float32),
        ],
        compiler_params=pltpu.CompilerParams(vmem_limit_bytes=2 << 20),
        name="final",
    )(place, total, image, basis)


def body(coefficients, tensor_blocks, basis_rows):
    coefficients = pltpu.with_memory_space_constraint(coefficients, pltpu.HBM)
    place = jnp.stack([lax.axis_index(axis) for axis in AXES]).astype(jnp.int32)

    own = tensor_blocks.reshape(K, 2 * HALF)
    across = move(own, FROM_ZH)
    both = jnp.stack([own, across])
    a, b = both[:, :, :HALF], both[:, :, HALF:]
    moved = [move(a, from_x(s)) for s in (1, 2, 3)] + [move(b, from_y(s)) for s in (1, 2, 3)]
    *moved, coefficients = lax.optimization_barrier((*moved, coefficients))
    loaded = load(coefficients)
    a = jnp.concatenate([a] + moved[:3])
    b = jnp.concatenate([b] + moved[3:])
    pieces_b = {0: b}
    for s in (2, 3, 1):
        pieces_b[s] = move(b, from_x(s))
    pieces_a = {0: a}
    for s in (2, 3, 1):
        pieces_a[s] = move(a, from_y(s))

    part = image_call(first_half_kernel, "image_a", ROWS, place, *[pieces_a[s] for s in range(4)], loaded)
    pieces = [pieces_b[s] for s in range(4)]
    part = image_call(
        second_half_kernel, "image_b", ROWS + 2 * OWN, place, *pieces, loaded, part, basis_rows
    )
    part = pair(place, part, move(part, FROM_CORE))
    image, total = products(place, part, move(part, FROM_ZL))
    total = total + move(total, FROM_Z)
    total = jnp.broadcast_to(total, (XS * YS, *total.shape))
    total = lax.all_to_all(total, ("x", "y"), 0, 0, tiled=True)
    return tuple(final(place, total, image, basis_rows))


def solution(mesh):
    mesh = Mesh(mesh.devices.reshape(XS, YS, 2, 2, 2), AXES)
    wide, narrow = AXES[:3], AXES[3:]
    in_specs = (P(None, wide, narrow), P(None, wide, narrow), P(None, AXES))
    out_specs = (P(None, AXES), P(), P())
    return jax.shard_map(body, mesh=mesh, in_specs=in_specs, out_specs=out_specs, check_vma=False)
```

```python
import functools

import jax
import jax.numpy as jnp
from jax import lax
from jax.experimental import pallas as pl
from jax.experimental.pallas import tpu as pltpu
from jax.sharding import Mesh, PartitionSpec as P

N = 8192
K = 8
R = 32
XS = 4
YS = 4
C = 2048
ROWS = 256
OWN = 64
AXES = ("x", "y", "zh", "zl", "core")
HI = lax.Precision.HIGHEST
NT = (((1,), (1,)), ((), ()))
NN = (((1,), (0,)), ((), ()))
VM = pl.BlockSpec(memory_space=pltpu.VMEM)
SM = pl.BlockSpec(memory_space=pltpu.SMEM)


def flat(x, y, zh, zl, core):
    return ((x * YS + y) * 2 + zh) * 4 + zl * 2 + core


def sources(source_of):
    pairs = []
    for x in range(XS):
        for y in range(YS):
            for zh in range(2):
                for zl in range(2):
                    for core in range(2):
                        here = (x, y, zh, zl, core)
                        pairs.append((flat(*source_of(*here)), flat(*here)))
    return pairs


def ring(step, x_core):
    def source(x, y, zh, zl, core):
        if core == x_core:
            return (x + step) % XS, y, zh, zl, core
        return x, (y + step) % YS, zh, zl, core

    return sources(source)


FROM_ZH = sources(lambda x, y, zh, zl, core: (x, y, 1 - zh, zl, core))
FROM_CORE = sources(lambda x, y, zh, zl, core: (x, y, zh, zl, 1 - core))

def along_z(step):
    def source(x, y, zh, zl, core):
        z = (zh * 2 + zl + step) % 4
        return x, y, z // 2, z % 2, 1 - core

    return sources(source)


def move(value, pairs):
    return lax.ppermute(value, AXES, pairs)


def split(value):
    high = value.astype(jnp.bfloat16)
    low = (value - high.astype(jnp.float32)).astype(jnp.bfloat16)
    return high, low


def load_kernel(source_ref, out_ref, sem):
    copy = pltpu.make_async_copy(source_ref, out_ref, sem)
    copy.start()
    copy.wait()


def load(coefficients):
    return pl.pallas_call(
        load_kernel,
        in_specs=[pl.BlockSpec(memory_space=pltpu.HBM)],
        out_specs=VM,
        out_shape=pltpu.VMEM(coefficients.shape, jnp.float32),
        scratch_shapes=[pltpu.SemaphoreType.DMA],
        compiler_params=pltpu.CompilerParams(vmem_limit_bytes=1 << 20),
        name="load",
    )(coefficients)


def image_kernel(place_ref, *refs):
    pieces, (block, basis_ref, out_ref, held) = refs[:8], refs[8:]
    total = None
    for k in range(K):
        rows = jnp.concatenate([piece[:, k, :] for piece in pieces], axis=0)
        rows_high, rows_low = split(rows)
        both = jnp.concatenate([rows_high, rows_low], axis=0)
        high, low = split(block[k])
        main = lax.dot_general(both, high, NT, preferred_element_type=jnp.float32)
        rest = lax.dot_general(rows_high, low, NT, preferred_element_type=jnp.float32)
        part = main[:R] + main[R:] + rest
        total = part if total is None else total + part
    held[...] = total
    x0, y0, zh0, core = place_ref[0], place_ref[1], place_ref[2], place_ref[4]
    for x in range(XS):
        for y in range(YS):
            for zh in range(2):
                dx = (x - x0 + XS) % XS
                dy = (y - y0 + YS) % YS
                dz = (zh + zh0) % 2
                slot = dz * 16 + jnp.where(core == 0, dy * 4 + dx, dx * 4 + dy)
                row = (x * YS + y) * 2 + zh
                out_ref[row : row + 1, 0:ROWS] = held[pl.ds(slot, 1), :]
    out_ref[:, ROWS : ROWS + OWN] = basis_ref[...]
    out_ref[:, ROWS + OWN :] = jnp.zeros_like(basis_ref)


def image_part(place, pieces, block, basis):
    return pl.pallas_call(
        image_kernel,
        in_specs=[SM] + [VM] * (len(pieces) + 2),
        out_specs=VM,
        out_shape=jax.ShapeDtypeStruct((R, ROWS + 2 * OWN), jnp.float32),
        scratch_shapes=[pltpu.VMEM((R, ROWS), jnp.float32)],
        compiler_params=pltpu.CompilerParams(vmem_limit_bytes=6 << 20),
        name="image",
    )(place, *pieces, block, basis)


def in_order(second, mine, other):
    return jnp.concatenate([jnp.where(second, other, mine), jnp.where(second, mine, other)], axis=1)


def pair_kernel(place_ref, mine_ref, other_ref, out_ref):
    out_ref[:, 0:ROWS] = mine_ref[:, 0:ROWS] + other_ref[:, 0:ROWS]
    own = slice(ROWS, ROWS + OWN)
    out_ref[:, ROWS:] = in_order(place_ref[4] == 1, mine_ref[:, own], other_ref[:, own])


def pair(place, mine, other):
    return pl.pallas_call(
        pair_kernel,
        in_specs=[SM, VM, VM],
        out_specs=VM,
        out_shape=jax.ShapeDtypeStruct(mine.shape, jnp.float32),
        compiler_params=pltpu.CompilerParams(vmem_limit_bytes=2 << 20),
        name="pair",
    )(place, mine, other)


def products_kernel(place_ref, *refs):
    parts, (image_ref, products_ref, held) = refs[:4], refs[4:]
    zh = place_ref[2]
    z = zh * 2 + place_ref[3]
    for step, part in enumerate(parts):
        held[pl.ds((z + step) % 4, 1)] = part[...][None]
    images = [held[2 * h, :, 0:ROWS] + held[2 * h + 1, :, 0:ROWS] for h in range(2)]
    image_ref[...] = jnp.where(zh == 0, images[0], images[1])
    image = jnp.concatenate(images, axis=1)
    basis = jnp.concatenate([held[i, :, ROWS:] for i in range(4)], axis=1)
    both = jnp.concatenate([image, basis], axis=0)
    of_image = lax.dot_general(image, both, NT, precision=HI, preferred_element_type=jnp.float32)
    of_basis = lax.dot_general(basis, both, NT, precision=HI, preferred_element_type=jnp.float32)
    products_ref[...] = jnp.concatenate([of_image, of_basis], axis=1)


def products(place, parts):
    return pl.pallas_call(
        products_kernel,
        in_specs=[SM] + [VM] * 4,
        out_specs=[VM] * 2,
        out_shape=[
            jax.ShapeDtypeStruct((R, ROWS), jnp.float32),
            jax.ShapeDtypeStruct((R, 4 * R), jnp.float32),
        ],
        scratch_shapes=[pltpu.VMEM((4, *parts[0].shape), jnp.float32)],
        compiler_params=pltpu.CompilerParams(vmem_limit_bytes=2 << 20),
        name="products",
    )(place, *parts)


def eliminate(work):
    lane = lax.broadcasted_iota(jnp.int32, (1, 4 * R), 1)
    done = []
    for k in range(0, R, 8):
        columns = [jnp.broadcast_to(work[:, k + m : k + m + 1], work.shape) for m in range(8)]
        rows = [work[k + m : k + m + 1, :] for m in range(8)]
        update = jnp.zeros_like(work)
        for m in range(8):
            at = k + m
            scale = lax.rsqrt(columns[m][at : at + 1, :])
            unit = rows[m] * scale
            column = columns[m] * scale
            done.append(jnp.where(lane >= at, unit, 0.0))
            for t in range(m + 1, 8):
                factor = columns[t][at : at + 1, :] * scale
                rows[t] = rows[t] - column[k + t : k + t + 1, :] * unit
                columns[t] = columns[t] - column * factor
            update = update + column * unit
        work = work - update
    return jnp.concatenate(done, axis=0)


def final_kernel(place_ref, products_ref, image_ref, basis_ref, new_ref, projection_ref, factor_ref):
    dot = functools.partial(lax.dot_general, precision=HI, preferred_element_type=jnp.float32)
    total = products_ref[0]
    for chip in range(1, XS * YS):
        total = total + products_ref[chip]
    squares = total[:, 0:R]
    first_t = total[:, R : 2 * R]
    first = total[:, 2 * R : 3 * R]
    basis_gram = total[:, 3 * R : 4 * R]
    projection = 2.0 * first - dot(basis_gram, first, NN)
    projection_t = 2.0 * first_t - dot(first_t, basis_gram, NN)
    projection_ref[...] = projection
    left = first - dot(basis_gram, projection, NN)
    gram = (squares - dot(first_t, projection, NN) - dot(projection_t, left, NN)) / N
    narrow = place_ref[3] * 2 + place_ref[4]
    own = image_ref[:, 0:64]
    for n in range(1, 4):
        own = jnp.where(narrow == n, image_ref[:, n * 64 : (n + 1) * 64], own)
    twice = own - dot(projection_t, basis_ref[...], NN)
    work = jnp.concatenate([gram, jnp.zeros((R, R), jnp.float32), twice], axis=1)
    rows = eliminate(work)
    factor_ref[...] = rows[:, 0:R].T
    new_ref[...] = rows[:, 2 * R : 4 * R]


def final(place, total, image, basis):
    return pl.pallas_call(
        final_kernel,
        in_specs=[SM] + [VM] * 3,
        out_specs=[VM] * 3,
        out_shape=[
            jax.ShapeDtypeStruct(basis.shape, jnp.float32),
            jax.ShapeDtypeStruct((R, R), jnp.float32),
            jax.ShapeDtypeStruct((R, R), jnp.float32),
        ],
        compiler_params=pltpu.CompilerParams(vmem_limit_bytes=2 << 20),
        name="final",
    )(place, total, image, basis)


def body(coefficients, tensor_blocks, basis_rows):
    coefficients = pltpu.with_memory_space_constraint(coefficients, pltpu.HBM)
    place = jnp.stack([lax.axis_index(axis) for axis in AXES]).astype(jnp.int32)

    own = tensor_blocks.reshape(K, C)
    moved = [move(own, ring(step, 0)) for step in (1, 2, 3)]
    row = jnp.stack(lax.optimization_barrier([own, *moved]))
    across = move(row, FROM_ZH)
    coefficients, across = lax.optimization_barrier((coefficients, across))
    loaded = load(coefficients)
    pieces = []
    for blocks in (row, across):
        pieces += [blocks] + [move(blocks, ring(step, 1)) for step in (1, 2, 3)]

    part = image_part(place, pieces, loaded, basis_rows)
    part = pair(place, part, move(part, FROM_CORE))
    image, total = products(place, [part] + [move(part, along_z(step)) for step in (1, 2, 3)])
    total = jnp.broadcast_to(total, (XS * YS, *total.shape))
    total = lax.all_to_all(total, ("x", "y"), 0, 0, tiled=True)
    return tuple(final(place, total, image, basis_rows))


def solution(mesh):
    mesh = Mesh(mesh.devices.reshape(XS, YS, 2, 2, 2), AXES)
    wide, narrow = AXES[:3], AXES[3:]
    in_specs = (P(None, wide, narrow), P(None, wide, narrow), P(None, AXES))
    out_specs = (P(None, AXES), P(), P())
    return jax.shard_map(body, mesh=mesh, in_specs=in_specs, out_specs=out_specs, check_vma=False)
```

```python
import functools

import jax
import jax.numpy as jnp
from jax import lax
from jax.experimental import pallas as pl
from jax.experimental.pallas import tpu as pltpu
from jax.sharding import Mesh, PartitionSpec as P

N = 8192
K = 8
R = 32
XS = 4
YS = 4
C = 2048
ROWS = 256
RB = 128
OWN = 64
AXES = ("x", "y", "zh", "zl", "core")
HI = lax.Precision.HIGHEST
NT = (((1,), (1,)), ((), ()))
NN = (((1,), (0,)), ((), ()))
VM = pl.BlockSpec(memory_space=pltpu.VMEM)
SM = pl.BlockSpec(memory_space=pltpu.SMEM)


def flat(x, y, zh, zl, core):
    return ((x * YS + y) * 2 + zh) * 4 + zl * 2 + core


def sources(source_of):
    pairs = []
    for x in range(XS):
        for y in range(YS):
            for zh in range(2):
                for zl in range(2):
                    for core in range(2):
                        here = (x, y, zh, zl, core)
                        pairs.append((flat(*source_of(*here)), flat(*here)))
    return pairs


def ring(step, x_core):
    def source(x, y, zh, zl, core):
        if core == x_core:
            return (x + step) % XS, y, zh, zl, core
        return x, (y + step) % YS, zh, zl, core

    return sources(source)


FROM_ZH = sources(lambda x, y, zh, zl, core: (x, y, 1 - zh, zl, core))
FROM_CORE = sources(lambda x, y, zh, zl, core: (x, y, zh, zl, 1 - core))

def along_z(step):
    def source(x, y, zh, zl, core):
        z = (zh * 2 + zl + step) % 4
        return x, y, z // 2, z % 2, 1 - core

    return sources(source)


def move(value, pairs):
    return lax.ppermute(value, AXES, pairs)


def split(value):
    high = value.astype(jnp.bfloat16)
    low = (value - high.astype(jnp.float32)).astype(jnp.bfloat16)
    return high, low


def load_kernel(source_ref, out_ref, sem):
    copy = pltpu.make_async_copy(source_ref, out_ref, sem)
    copy.start()
    copy.wait()


def load(coefficients):
    return pl.pallas_call(
        load_kernel,
        in_specs=[pl.BlockSpec(memory_space=pltpu.HBM)],
        out_specs=VM,
        out_shape=pltpu.VMEM(coefficients.shape, jnp.float32),
        scratch_shapes=[pltpu.SemaphoreType.DMA],
        compiler_params=pltpu.CompilerParams(vmem_limit_bytes=1 << 20),
        name="load",
    )(coefficients)


def image_kernel(place_ref, *refs):
    pieces, (block, basis_ref, out_ref, held, split_rows) = refs[:8], refs[8:]
    for k in range(K):
        high, low = split(jnp.concatenate([piece[:, k, :] for piece in pieces], axis=0))
        split_rows[0:R, k * C : (k + 1) * C] = high
        split_rows[R : 2 * R, k * C : (k + 1) * C] = low
    for r in range(0, ROWS, RB):
        total = None
        for k in range(K):
            high, low = split(block[k, r : r + RB, :])
            both = jnp.concatenate([high, low], axis=0)
            part = lax.dot_general(both, split_rows[:, k * C : (k + 1) * C], NT, preferred_element_type=jnp.float32)
            total = part if total is None else total + part
        total = total.T
        held[:, r : r + RB] = (total[:R, :RB] + total[R:, RB:]) + (total[R:, :RB] + total[:R, RB:])
    x0, y0, zh0, core = place_ref[0], place_ref[1], place_ref[2], place_ref[4]
    for x in range(XS):
        for y in range(YS):
            for zh in range(2):
                dx = (x - x0 + XS) % XS
                dy = (y - y0 + YS) % YS
                slot = (zh ^ zh0) * 16 + jnp.where(core == 0, dy * 4 + dx, dx * 4 + dy)
                row = (x * YS + y) * 2 + zh
                out_ref[row : row + 1, 0:ROWS] = held[pl.ds(slot, 1), :]
    out_ref[:, ROWS : ROWS + OWN] = basis_ref[...]
    out_ref[:, ROWS + OWN :] = jnp.zeros_like(basis_ref)


def image_part(place, pieces, block, basis):
    return pl.pallas_call(
        image_kernel,
        in_specs=[SM] + [VM] * (len(pieces) + 2),
        out_specs=VM,
        out_shape=jax.ShapeDtypeStruct((R, ROWS + 2 * OWN), jnp.float32),
        scratch_shapes=[pltpu.VMEM((R, ROWS), jnp.float32), pltpu.VMEM((2 * R, K * C), jnp.bfloat16)],
        compiler_params=pltpu.CompilerParams(vmem_limit_bytes=8 << 20),
        name="image",
    )(place, *pieces, block, basis)


def in_order(second, mine, other):
    return jnp.concatenate([jnp.where(second, other, mine), jnp.where(second, mine, other)], axis=1)


def pair(second, mine, other):
    own = slice(ROWS, ROWS + OWN)
    image = mine[:, :ROWS] + other[:, :ROWS]
    return jnp.concatenate([image, in_order(second, mine[:, own], other[:, own])], axis=1)


def products_kernel(place_ref, *refs):
    parts, (image_ref, products_ref, held) = refs[:4], refs[4:]
    zh = place_ref[2]
    z = zh * 2 + place_ref[3]
    for step, part in enumerate(parts):
        held[pl.ds((z + step) % 4, 1)] = part[...][None]
    images = [held[2 * h, :, 0:ROWS] + held[2 * h + 1, :, 0:ROWS] for h in range(2)]
    image_ref[...] = jnp.where(zh == 0, images[0], images[1])
    image = jnp.concatenate(images, axis=1)
    basis = jnp.concatenate([held[i, :, ROWS:] for i in range(4)], axis=1)
    both = jnp.concatenate([image, basis], axis=0)
    of_image = lax.dot_general(image, both, NT, precision=HI, preferred_element_type=jnp.float32)
    of_basis = lax.dot_general(basis, both, NT, precision=HI, preferred_element_type=jnp.float32)
    products_ref[...] = jnp.concatenate([of_image, of_basis], axis=1)


def products(place, parts):
    return pl.pallas_call(
        products_kernel,
        in_specs=[SM] + [VM] * 4,
        out_specs=[VM] * 2,
        out_shape=[
            jax.ShapeDtypeStruct((R, ROWS), jnp.float32),
            jax.ShapeDtypeStruct((R, 4 * R), jnp.float32),
        ],
        scratch_shapes=[pltpu.VMEM((4, *parts[0].shape), jnp.float32)],
        compiler_params=pltpu.CompilerParams(vmem_limit_bytes=2 << 20),
        name="products",
    )(place, *parts)


def eliminate(work):
    lane = lax.broadcasted_iota(jnp.int32, (1, 4 * R), 1)
    done = []
    for k in range(0, R, 8):
        columns = [jnp.broadcast_to(work[:, k + m : k + m + 1], work.shape) for m in range(8)]
        rows = [work[k + m : k + m + 1, :] for m in range(8)]
        update = jnp.zeros_like(work)
        for m in range(8):
            at = k + m
            scale = lax.rsqrt(columns[m][at : at + 1, :])
            unit = rows[m] * scale
            column = columns[m] * scale
            done.append(jnp.where(lane >= at, unit, 0.0))
            for t in range(m + 1, 8):
                factor = columns[t][at : at + 1, :] * scale
                rows[t] = rows[t] - column[k + t : k + t + 1, :] * unit
                columns[t] = columns[t] - column * factor
            update = update + column * unit
        work = work - update
    return jnp.concatenate(done, axis=0)


def final_kernel(place_ref, products_ref, image_ref, basis_ref, new_ref, projection_ref, factor_ref):
    dot = functools.partial(lax.dot_general, precision=HI, preferred_element_type=jnp.float32)
    total = products_ref[0]
    for chip in range(1, XS * YS):
        total = total + products_ref[chip]
    squares = total[:, 0:R]
    first_t = total[:, R : 2 * R]
    first = total[:, 2 * R : 3 * R]
    basis_gram = total[:, 3 * R : 4 * R]
    projection = 2.0 * first - dot(basis_gram, first, NN)
    projection_t = 2.0 * first_t - dot(first_t, basis_gram, NN)
    projection_ref[...] = projection
    left = first - dot(basis_gram, projection, NN)
    gram = (squares - dot(first_t, projection, NN) - dot(projection_t, left, NN)) / N
    narrow = place_ref[3] * 2 + place_ref[4]
    own = image_ref[:, 0:64]
    for n in range(1, 4):
        own = jnp.where(narrow == n, image_ref[:, n * 64 : (n + 1) * 64], own)
    twice = own - dot(projection_t, basis_ref[...], NN)
    work = jnp.concatenate([gram, jnp.zeros((R, R), jnp.float32), twice], axis=1)
    rows = eliminate(work)
    factor_ref[...] = rows[:, 0:R].T
    new_ref[...] = rows[:, 2 * R : 4 * R]


def final(place, total, image, basis):
    return pl.pallas_call(
        final_kernel,
        in_specs=[SM] + [VM] * 3,
        out_specs=[VM] * 3,
        out_shape=[
            jax.ShapeDtypeStruct(basis.shape, jnp.float32),
            jax.ShapeDtypeStruct((R, R), jnp.float32),
            jax.ShapeDtypeStruct((R, R), jnp.float32),
        ],
        compiler_params=pltpu.CompilerParams(vmem_limit_bytes=2 << 20),
        name="final",
    )(place, total, image, basis)


def body(coefficients, tensor_blocks, basis_rows):
    coefficients = pltpu.with_memory_space_constraint(coefficients, pltpu.HBM)
    place = jnp.stack([lax.axis_index(axis) for axis in AXES]).astype(jnp.int32)

    own = tensor_blocks.reshape(K, C)
    moved = [move(own, ring(step, 0)) for step in (1, 2, 3)]
    row = jnp.stack(lax.optimization_barrier([own, *moved]))
    across = move(row, FROM_ZH)
    coefficients, across = lax.optimization_barrier((coefficients, across))
    loaded = load(coefficients)
    pieces = []
    for blocks in (row, across):
        pieces += [blocks] + [move(blocks, ring(step, 1)) for step in (1, 2, 3)]

    part = image_part(place, pieces, loaded, basis_rows)
    part = pair(place[4] == 1, part, move(part, FROM_CORE))
    image, total = products(place, [part] + [move(part, along_z(step)) for step in (1, 2, 3)])
    total = jnp.broadcast_to(total, (XS * YS, *total.shape))
    total = lax.all_to_all(total, ("x", "y"), 0, 0, tiled=True)
    return tuple(final(place, total, image, basis_rows))


def solution(mesh):
    mesh = Mesh(mesh.devices.reshape(XS, YS, 2, 2, 2), AXES)
    wide, narrow = AXES[:3], AXES[3:]
    in_specs = (P(None, wide, narrow), P(None, wide, narrow), P(None, AXES))
    out_specs = (P(None, AXES), P(), P())
    return jax.shard_map(body, mesh=mesh, in_specs=in_specs, out_specs=out_specs, check_vma=False)
```

```python
import functools

import jax
import jax.numpy as jnp
from jax import lax
from jax.experimental import pallas as pl
from jax.experimental.pallas import tpu as pltpu
from jax.sharding import Mesh, PartitionSpec as P

N = 8192
K = 8
R = 32
XS = 4
YS = 4
C = 2048
ROWS = 256
RB = 128
OWN = 64
AXES = ("x", "y", "zh", "zl", "core")
HI = lax.Precision.HIGHEST
NT = (((1,), (1,)), ((), ()))
NN = (((1,), (0,)), ((), ()))
VM = pl.BlockSpec(memory_space=pltpu.VMEM)
SM = pl.BlockSpec(memory_space=pltpu.SMEM)


def flat(x, y, zh, zl, core):
    return ((x * YS + y) * 2 + zh) * 4 + zl * 2 + core


def sources(source_of):
    pairs = []
    for x in range(XS):
        for y in range(YS):
            for zh in range(2):
                for zl in range(2):
                    for core in range(2):
                        here = (x, y, zh, zl, core)
                        pairs.append((flat(*source_of(*here)), flat(*here)))
    return pairs


def ring(step, x_core):
    def source(x, y, zh, zl, core):
        if core == x_core:
            return (x + step) % XS, y, zh, zl, core
        return x, (y + step) % YS, zh, zl, core

    return sources(source)


FROM_ZH = sources(lambda x, y, zh, zl, core: (x, y, 1 - zh, zl, core))
FROM_CORE = sources(lambda x, y, zh, zl, core: (x, y, zh, zl, 1 - core))

def along_z(step):
    def source(x, y, zh, zl, core):
        z = (zh * 2 + zl + step) % 4
        return x, y, z // 2, z % 2, 1 - core

    return sources(source)


def move(value, pairs):
    return lax.ppermute(value, AXES, pairs)


def split(value):
    high = value.astype(jnp.bfloat16)
    low = (value - high.astype(jnp.float32)).astype(jnp.bfloat16)
    return high, low


def load_kernel(source_ref, out_ref, sem):
    copy = pltpu.make_async_copy(source_ref, out_ref, sem)
    copy.start()
    copy.wait()


def load(coefficients):
    return pl.pallas_call(
        load_kernel,
        in_specs=[pl.BlockSpec(memory_space=pltpu.HBM)],
        out_specs=VM,
        out_shape=pltpu.VMEM(coefficients.shape, jnp.float32),
        scratch_shapes=[pltpu.SemaphoreType.DMA],
        compiler_params=pltpu.CompilerParams(vmem_limit_bytes=1 << 20),
        name="load",
    )(coefficients)


def image_kernel(place_ref, *refs):
    pieces, (block, basis_ref, out_ref, held, split_rows) = refs[:8], refs[8:]
    for k in range(K):
        high, low = split(jnp.concatenate([piece[:, k, :] for piece in pieces], axis=0))
        split_rows[0:R, k * C : (k + 1) * C] = high
        split_rows[R : 2 * R, k * C : (k + 1) * C] = low
    for r in range(0, ROWS, RB):
        total = None
        for k in range(K):
            high, low = split(block[k, r : r + RB, :])
            both = jnp.concatenate([high, low], axis=0)
            part = lax.dot_general(both, split_rows[:, k * C : (k + 1) * C], NT, preferred_element_type=jnp.float32)
            total = part if total is None else total + part
        total = total.T
        held[:, r : r + RB] = (total[:R, :RB] + total[R:, RB:]) + (total[R:, :RB] + total[:R, RB:])
    x0, y0, zh0, core = place_ref[0], place_ref[1], place_ref[2], place_ref[4]
    for x in range(XS):
        for y in range(YS):
            for zh in range(2):
                dx = (x - x0 + XS) % XS
                dy = (y - y0 + YS) % YS
                slot = (zh ^ zh0) * 16 + jnp.where(core == 0, dy * 4 + dx, dx * 4 + dy)
                row = (x * YS + y) * 2 + zh
                out_ref[row : row + 1, 0:ROWS] = held[pl.ds(slot, 1), :]
    out_ref[:, ROWS : ROWS + OWN] = basis_ref[...]
    out_ref[:, ROWS + OWN :] = jnp.zeros_like(basis_ref)


def image_part(place, pieces, block, basis):
    return pl.pallas_call(
        image_kernel,
        in_specs=[SM] + [VM] * (len(pieces) + 2),
        out_specs=VM,
        out_shape=jax.ShapeDtypeStruct((R, ROWS + 2 * OWN), jnp.float32),
        scratch_shapes=[pltpu.VMEM((R, ROWS), jnp.float32), pltpu.VMEM((2 * R, K * C), jnp.bfloat16)],
        compiler_params=pltpu.CompilerParams(vmem_limit_bytes=8 << 20),
        name="image",
    )(place, *pieces, block, basis)


def in_order(second, mine, other):
    return jnp.concatenate([jnp.where(second, other, mine), jnp.where(second, mine, other)], axis=1)


def pair(second, mine, other):
    own = slice(ROWS, ROWS + OWN)
    image = mine[:, :ROWS] + other[:, :ROWS]
    return jnp.concatenate([image, in_order(second, mine[:, own], other[:, own])], axis=1)


def products_kernel(place_ref, *refs):
    parts, (image_ref, products_ref, held) = refs[:4], refs[4:]
    zh = place_ref[2]
    z = zh * 2 + place_ref[3]
    for step, part in enumerate(parts):
        held[pl.ds((z + step) % 4, 1)] = part[...][None]
    images = [held[2 * h, :, 0:ROWS] + held[2 * h + 1, :, 0:ROWS] for h in range(2)]
    image_ref[...] = jnp.where(zh == 0, images[0], images[1])
    image = jnp.concatenate(images, axis=1)
    basis = jnp.concatenate([held[i, :, ROWS:] for i in range(4)], axis=1)
    both = jnp.concatenate([image, basis], axis=0)
    of_image = lax.dot_general(image, both, NT, precision=HI, preferred_element_type=jnp.float32)
    of_basis = lax.dot_general(basis, both, NT, precision=HI, preferred_element_type=jnp.float32)
    products_ref[...] = jnp.concatenate([of_image, of_basis], axis=1)


def products(place, parts):
    return pl.pallas_call(
        products_kernel,
        in_specs=[SM] + [VM] * 4,
        out_specs=[VM] * 2,
        out_shape=[
            jax.ShapeDtypeStruct((R, ROWS), jnp.float32),
            jax.ShapeDtypeStruct((R, 4 * R), jnp.float32),
        ],
        scratch_shapes=[pltpu.VMEM((4, *parts[0].shape), jnp.float32)],
        compiler_params=pltpu.CompilerParams(vmem_limit_bytes=2 << 20),
        name="products",
    )(place, *parts)


def eliminate(work):
    lane = lax.broadcasted_iota(jnp.int32, (1, 4 * R), 1)
    done = []
    for k in range(0, R, 8):
        columns = [jnp.broadcast_to(work[:, k + m : k + m + 1], work.shape) for m in range(8)]
        rows = [work[k + m : k + m + 1, :] for m in range(8)]
        update = jnp.zeros_like(work)
        for m in range(8):
            at = k + m
            scale = lax.rsqrt(columns[m][at : at + 1, :])
            unit = rows[m] * scale
            column = columns[m] * scale
            done.append(jnp.where(lane >= at, unit, 0.0))
            for t in range(m + 1, 8):
                factor = columns[t][at : at + 1, :] * scale
                rows[t] = rows[t] - column[k + t : k + t + 1, :] * unit
                columns[t] = columns[t] - column * factor
            update = update + column * unit
        work = work - update
    return jnp.concatenate(done, axis=0)


def final_kernel(place_ref, products_ref, image_ref, basis_ref, new_ref, projection_ref, factor_ref):
    dot = functools.partial(lax.dot_general, precision=HI, preferred_element_type=jnp.float32)
    total = products_ref[0]
    for chip in range(1, XS * YS):
        total = total + products_ref[chip]
    squares = total[:, 0:R]
    first_t = total[:, R : 2 * R]
    first = total[:, 2 * R : 3 * R]
    basis_gram = total[:, 3 * R : 4 * R]
    projection = 2.0 * first - dot(basis_gram, first, NN)
    projection_t = 2.0 * first_t - dot(first_t, basis_gram, NN)
    projection_ref[...] = projection
    left = first - dot(basis_gram, projection, NN)
    gram = (squares - dot(first_t, projection, NN) - dot(projection_t, left, NN)) / N
    narrow = place_ref[3] * 2 + place_ref[4]
    own = image_ref[:, 0:64]
    for n in range(1, 4):
        own = jnp.where(narrow == n, image_ref[:, n * 64 : (n + 1) * 64], own)
    twice = own - dot(projection_t, basis_ref[...], NN)
    work = jnp.concatenate([gram, jnp.zeros((R, R), jnp.float32), twice], axis=1)
    rows = eliminate(work)
    factor_ref[...] = rows[:, 0:R].T
    new_ref[...] = rows[:, 2 * R : 4 * R]


def final(place, total, image, basis):
    return pl.pallas_call(
        final_kernel,
        in_specs=[SM] + [VM] * 3,
        out_specs=[VM] * 3,
        out_shape=[
            jax.ShapeDtypeStruct(basis.shape, jnp.float32),
            jax.ShapeDtypeStruct((R, R), jnp.float32),
            jax.ShapeDtypeStruct((R, R), jnp.float32),
        ],
        compiler_params=pltpu.CompilerParams(vmem_limit_bytes=2 << 20),
        name="final",
    )(place, total, image, basis)


def body(coefficients, tensor_blocks, basis_rows):
    coefficients = pltpu.with_memory_space_constraint(coefficients, pltpu.HBM)
    place = jnp.stack([lax.axis_index(axis) for axis in AXES]).astype(jnp.int32)

    own = tensor_blocks.reshape(K, C)
    own_across = move(own, FROM_ZH)
    moved = [move(own, ring(step, 0)) for step in (1, 2, 3)]
    own, *moved = lax.optimization_barrier([own, *moved])
    row = jnp.stack([own, *moved])
    across = move(jnp.stack(moved), FROM_ZH)
    far, one, three = [move(row, ring(step, 1)) for step in (2, 1, 3)]
    across = jnp.concatenate([own_across[None], across])
    far_across = move(far, FROM_ZH)
    coefficients, across = lax.optimization_barrier((coefficients, across))
    loaded = load(coefficients)
    one_across, three_across = [move(across, ring(step, 1)) for step in (1, 3)]
    pieces = [row, one, far, three, across, one_across, far_across, three_across]

    part = image_part(place, pieces, loaded, basis_rows)
    part = pair(place[4] == 1, part, move(part, FROM_CORE))
    image, total = products(place, [part] + [move(part, along_z(step)) for step in (1, 2, 3)])
    total = jnp.broadcast_to(total, (XS * YS, *total.shape))
    total = lax.all_to_all(total, ("x", "y"), 0, 0, tiled=True)
    return tuple(final(place, total, image, basis_rows))


def solution(mesh):
    mesh = Mesh(mesh.devices.reshape(XS, YS, 2, 2, 2), AXES)
    wide, narrow = AXES[:3], AXES[3:]
    in_specs = (P(None, wide, narrow), P(None, wide, narrow), P(None, AXES))
    out_specs = (P(None, AXES), P(), P())
    return jax.shard_map(body, mesh=mesh, in_specs=in_specs, out_specs=out_specs, check_vma=False)
```

```python
import functools

import jax
import jax.numpy as jnp
from jax import lax
from jax.experimental import pallas as pl
from jax.experimental.pallas import tpu as pltpu
from jax.sharding import Mesh, PartitionSpec as P

N = 8192
K = 8
R = 32
XS = 4
YS = 4
C = 2048
LANES = 16
ROWS = 256
RB = 128
OWN = 64
AXES = ("x", "y", "zh", "zl", "core")
HI = lax.Precision.HIGHEST
NT = (((1,), (1,)), ((), ()))
NN = (((1,), (0,)), ((), ()))
VM = pl.BlockSpec(memory_space=pltpu.VMEM)
SM = pl.BlockSpec(memory_space=pltpu.SMEM)


def flat(x, y, zh, zl, core):
    return ((x * YS + y) * 2 + zh) * 4 + zl * 2 + core


def sources(source_of):
    pairs = []
    for x in range(XS):
        for y in range(YS):
            for zh in range(2):
                for zl in range(2):
                    for core in range(2):
                        here = (x, y, zh, zl, core)
                        pairs.append((flat(*source_of(*here)), flat(*here)))
    return pairs


def ring(step, x_core):
    def source(x, y, zh, zl, core):
        if core == x_core:
            return (x + step) % XS, y, zh, zl, core
        return x, (y + step) % YS, zh, zl, core

    return sources(source)


FROM_ZH = sources(lambda x, y, zh, zl, core: (x, y, 1 - zh, zl, core))
FROM_CORE = sources(lambda x, y, zh, zl, core: (x, y, zh, zl, 1 - core))

def along_z(step):
    def source(x, y, zh, zl, core):
        z = (zh * 2 + zl + step) % 4
        return x, y, z // 2, z % 2, 1 - core

    return sources(source)


def move(value, pairs):
    return lax.ppermute(value, AXES, pairs)


def split(value):
    high = value.astype(jnp.bfloat16)
    low = (value - high.astype(jnp.float32)).astype(jnp.bfloat16)
    return high, low


def hold_kernel(source_ref, out_ref, sem):
    copy = pltpu.make_async_copy(source_ref, out_ref, sem)
    copy.start()
    copy.wait()


def hold(block):
    return pl.pallas_call(
        hold_kernel,
        in_specs=[pl.BlockSpec(memory_space=pltpu.HBM)],
        out_specs=VM,
        out_shape=jax.ShapeDtypeStruct(block.shape, jnp.float32),
        scratch_shapes=[pltpu.SemaphoreType.DMA],
        compiler_params=pltpu.CompilerParams(vmem_limit_bytes=1 << 20),
        name="hold",
    )(block)


def load_kernel(source_ref, out_ref, sem):
    copy = pltpu.make_async_copy(source_ref, out_ref, sem)
    copy.start()
    copy.wait()


def load(coefficients):
    return pl.pallas_call(
        load_kernel,
        in_specs=[pl.BlockSpec(memory_space=pltpu.HBM)],
        out_specs=VM,
        out_shape=pltpu.VMEM(coefficients.shape, jnp.float32),
        scratch_shapes=[pltpu.SemaphoreType.DMA],
        compiler_params=pltpu.CompilerParams(vmem_limit_bytes=1 << 20),
        name="load",
    )(coefficients)


def image_kernel(place_ref, *refs):
    pieces, (block, basis_ref, out_ref, held, split_rows) = refs[:8], refs[8:]
    for k in range(K):
        for j in range(LANES):
            at = k * LANES + j
            rows = [piece[:, at, :] for piece in pieces]
            high, low = split(jnp.concatenate(rows, axis=0))
            split_rows[:, at * 128 : (at + 1) * 128] = jnp.concatenate([high, low], axis=0)
    for r in range(0, ROWS, RB):
        total = None
        for k in range(K):
            high, low = split(block[k, r : r + RB, :])
            both = jnp.concatenate([high, low], axis=0)
            part = lax.dot_general(both, split_rows[:, k * C : (k + 1) * C], NT, preferred_element_type=jnp.float32)
            total = part if total is None else total + part
        total = total.T
        held[:, r : r + RB] = (total[:R, :RB] + total[R:, RB:]) + (total[R:, :RB] + total[:R, RB:])
    x0, y0, zh0, core = place_ref[0], place_ref[1], place_ref[2], place_ref[4]
    for x in range(XS):
        for y in range(YS):
            for zh in range(2):
                dx = (x - x0 + XS) % XS
                dy = (y - y0 + YS) % YS
                slot = (zh ^ zh0) * 16 + jnp.where(core == 1, dy * 4 + dx, dx * 4 + dy)
                row = (x * YS + y) * 2 + zh
                out_ref[row : row + 1, 0:ROWS] = held[pl.ds(slot, 1), :]
    out_ref[:, ROWS : ROWS + OWN] = basis_ref[...]
    out_ref[:, ROWS + OWN :] = jnp.zeros_like(basis_ref)


def image_part(place, pieces, block, basis):
    return pl.pallas_call(
        image_kernel,
        in_specs=[SM] + [VM] * (len(pieces) + 2),
        out_specs=VM,
        out_shape=jax.ShapeDtypeStruct((R, ROWS + 2 * OWN), jnp.float32),
        scratch_shapes=[pltpu.VMEM((R, ROWS), jnp.float32), pltpu.VMEM((2 * R, K * C), jnp.bfloat16)],
        compiler_params=pltpu.CompilerParams(vmem_limit_bytes=8 << 20),
        name="image",
    )(place, *pieces, block, basis)


def in_order(second, mine, other):
    return jnp.concatenate([jnp.where(second, other, mine), jnp.where(second, mine, other)], axis=1)


def pair(second, mine, other):
    own = slice(ROWS, ROWS + OWN)
    image = mine[:, :ROWS] + other[:, :ROWS]
    return jnp.concatenate([image, in_order(second, mine[:, own], other[:, own])], axis=1)


def products_kernel(place_ref, *refs):
    parts, (image_ref, products_ref, held) = refs[:4], refs[4:]
    zh = place_ref[2]
    z = zh * 2 + place_ref[3]
    for step, part in enumerate(parts):
        held[pl.ds((z + step) % 4, 1)] = part[...][None]
    images = [held[2 * h, :, 0:ROWS] + held[2 * h + 1, :, 0:ROWS] for h in range(2)]
    image_ref[...] = jnp.where(zh == 0, images[0], images[1])
    image = jnp.concatenate(images, axis=1)
    basis = jnp.concatenate([held[i, :, ROWS:] for i in range(4)], axis=1)
    both = jnp.concatenate([image, basis], axis=0)
    total = lax.dot_general(both, both, NT, precision=HI, preferred_element_type=jnp.float32)
    products_ref[...] = jnp.concatenate([total[:R], total[R:]], axis=1)


def products(place, parts):
    return pl.pallas_call(
        products_kernel,
        in_specs=[SM] + [VM] * 4,
        out_specs=[VM] * 2,
        out_shape=[
            jax.ShapeDtypeStruct((R, ROWS), jnp.float32),
            jax.ShapeDtypeStruct((R, 4 * R), jnp.float32),
        ],
        scratch_shapes=[pltpu.VMEM((4, *parts[0].shape), jnp.float32)],
        compiler_params=pltpu.CompilerParams(vmem_limit_bytes=2 << 20),
        name="products",
    )(place, *parts)


def eliminate(work):
    lane = lax.broadcasted_iota(jnp.int32, (1, 4 * R), 1)
    done = []
    for k in range(0, R, 8):
        columns = [jnp.broadcast_to(work[:, k + m : k + m + 1], work.shape) for m in range(8)]
        rows = [work[k + m : k + m + 1, :] for m in range(8)]
        update = jnp.zeros_like(work)
        for m in range(8):
            at = k + m
            scale = lax.rsqrt(columns[m][at : at + 1, :])
            unit = rows[m] * scale
            column = columns[m] * scale
            done.append(jnp.where(lane >= at, unit, 0.0))
            for t in range(m + 1, 8):
                factor = columns[t][at : at + 1, :] * scale
                rows[t] = rows[t] - column[k + t : k + t + 1, :] * unit
                columns[t] = columns[t] - column * factor
            update = update + column * unit
        work = work - update
    return jnp.concatenate(done, axis=0)


def final_kernel(place_ref, products_ref, image_ref, basis_ref, new_ref, projection_ref, factor_ref):
    dot = functools.partial(lax.dot_general, precision=HI, preferred_element_type=jnp.float32)
    total = products_ref[0]
    for chip in range(1, XS * YS):
        total = total + products_ref[chip]
    squares = total[:, 0:R]
    first_t = total[:, R : 2 * R]
    first = total[:, 2 * R : 3 * R]
    basis_gram = total[:, 3 * R : 4 * R]
    projection = 2.0 * first - dot(basis_gram, first, NN)
    projection_t = 2.0 * first_t - dot(first_t, basis_gram, NN)
    projection_ref[...] = projection
    left = first - dot(basis_gram, projection, NN)
    gram = (squares - dot(first_t, projection, NN) - dot(projection_t, left, NN)) / N
    narrow = place_ref[3] * 2 + place_ref[4]
    own = image_ref[:, 0:64]
    for n in range(1, 4):
        own = jnp.where(narrow == n, image_ref[:, n * 64 : (n + 1) * 64], own)
    twice = own - dot(projection_t, basis_ref[...], NN)
    work = jnp.concatenate([gram, jnp.zeros((R, R), jnp.float32), twice], axis=1)
    rows = eliminate(work)
    factor_ref[...] = rows[:, 0:R].T
    new_ref[...] = rows[:, 2 * R : 4 * R]


def final(place, total, image, basis):
    return pl.pallas_call(
        final_kernel,
        in_specs=[SM] + [VM] * 3,
        out_specs=[VM] * 3,
        out_shape=[
            jax.ShapeDtypeStruct(basis.shape, jnp.float32),
            jax.ShapeDtypeStruct((R, R), jnp.float32),
            jax.ShapeDtypeStruct((R, R), jnp.float32),
        ],
        compiler_params=pltpu.CompilerParams(vmem_limit_bytes=2 << 20),
        name="final",
    )(place, total, image, basis)


def body(coefficients, tensor_blocks, basis_rows):
    coefficients = pltpu.with_memory_space_constraint(coefficients, pltpu.HBM)
    place = jnp.stack([lax.axis_index(axis) for axis in AXES]).astype(jnp.int32)

    own = tensor_blocks.reshape(K * LANES, C // LANES)
    held_own = hold(own)
    moved = [move(own, ring(step, 1)) for step in (1, 2, 3)]
    held_own, *moved = lax.optimization_barrier([held_own, *moved])
    row = jnp.stack([held_own, *moved])
    across = move(row, FROM_ZH)
    far, one, three = [move(row, ring(step, 0)) for step in (2, 1, 3)]
    far_across = move(far, FROM_ZH)
    coefficients, across = lax.optimization_barrier((coefficients, across))
    loaded = load(coefficients)
    one_across, three_across = [move(across, ring(step, 0)) for step in (1, 3)]
    pieces = [row, one, far, three, across, one_across, far_across, three_across]

    part = image_part(place, pieces, loaded, basis_rows)
    part = pair(place[4] == 1, part, move(part, FROM_CORE))
    image, total = products(place, [part] + [move(part, along_z(step)) for step in (1, 2, 3)])
    total = jnp.broadcast_to(total, (XS * YS, *total.shape))
    total = lax.all_to_all(total, ("x", "y"), 0, 0, tiled=True)
    return tuple(final(place, total, image, basis_rows))


def solution(mesh):
    mesh = Mesh(mesh.devices.reshape(XS, YS, 2, 2, 2), AXES)
    wide, narrow = AXES[:3], AXES[3:]
    in_specs = (P(None, wide, narrow), P(None, wide, narrow), P(None, AXES))
    out_specs = (P(None, AXES), P(), P())
    return jax.shard_map(body, mesh=mesh, in_specs=in_specs, out_specs=out_specs, check_vma=False)
```

```python
import functools

import jax
import jax.numpy as jnp
from jax import lax
from jax.experimental import pallas as pl
from jax.experimental.pallas import tpu as pltpu
from jax.sharding import Mesh, PartitionSpec as P

N = 8192
K = 8
R = 32
XS = 4
YS = 4
C = 2048
LANES = 16
ROWS = 256
RB = 128
OWN = 64
AXES = ("x", "y", "zh", "zl", "core")
HI = lax.Precision.HIGHEST
NT = (((1,), (1,)), ((), ()))
NN = (((1,), (0,)), ((), ()))
VM = pl.BlockSpec(memory_space=pltpu.VMEM)
SM = pl.BlockSpec(memory_space=pltpu.SMEM)


def flat(x, y, zh, zl, core):
    return ((x * YS + y) * 2 + zh) * 4 + zl * 2 + core


def sources(source_of):
    pairs = []
    for x in range(XS):
        for y in range(YS):
            for zh in range(2):
                for zl in range(2):
                    for core in range(2):
                        here = (x, y, zh, zl, core)
                        pairs.append((flat(*source_of(*here)), flat(*here)))
    return pairs


def ring(step, x_core):
    def source(x, y, zh, zl, core):
        if core == x_core:
            return (x + step) % XS, y, zh, zl, core
        return x, (y + step) % YS, zh, zl, core

    return sources(source)


FROM_ZH = sources(lambda x, y, zh, zl, core: (x, y, 1 - zh, zl, core))
FROM_CORE = sources(lambda x, y, zh, zl, core: (x, y, zh, zl, 1 - core))

def along_z(step):
    def source(x, y, zh, zl, core):
        z = (zh * 2 + zl + step) % 4
        return x, y, z // 2, z % 2, 1 - core

    return sources(source)


def move(value, pairs):
    return lax.ppermute(value, AXES, pairs)


def split(value):
    high = value.astype(jnp.bfloat16)
    low = (value - high.astype(jnp.float32)).astype(jnp.bfloat16)
    return high, low


def hold_kernel(source_ref, out_ref, sem):
    copy = pltpu.make_async_copy(source_ref, out_ref, sem)
    copy.start()
    copy.wait()


def hold(block):
    return pl.pallas_call(
        hold_kernel,
        in_specs=[pl.BlockSpec(memory_space=pltpu.HBM)],
        out_specs=VM,
        out_shape=jax.ShapeDtypeStruct(block.shape, jnp.float32),
        scratch_shapes=[pltpu.SemaphoreType.DMA],
        compiler_params=pltpu.CompilerParams(vmem_limit_bytes=1 << 20),
        name="hold",
    )(block)


def load_kernel(source_ref, out_ref, sem):
    copy = pltpu.make_async_copy(source_ref, out_ref, sem)
    copy.start()
    copy.wait()


def load(coefficients):
    return pl.pallas_call(
        load_kernel,
        in_specs=[pl.BlockSpec(memory_space=pltpu.HBM)],
        out_specs=VM,
        out_shape=pltpu.VMEM(coefficients.shape, jnp.float32),
        scratch_shapes=[pltpu.SemaphoreType.DMA],
        compiler_params=pltpu.CompilerParams(vmem_limit_bytes=1 << 20),
        name="load",
    )(coefficients)


def image_kernel(place_ref, *refs):
    pieces, (block, basis_ref, out_ref, held, split_rows) = refs[:8], refs[8:]
    for k in range(K):
        tiles = []
        for at in range(k * LANES, (k + 1) * LANES):
            tiles.append(jnp.concatenate([piece[:, at, :] for piece in pieces], axis=0))
        high, low = split(jnp.concatenate(tiles, axis=1))
        split_rows[0:R, k * C : (k + 1) * C] = high
        split_rows[R : 2 * R, k * C : (k + 1) * C] = low
    for r in range(0, ROWS, RB):
        total = None
        for k in range(K):
            high, low = split(block[k, r : r + RB, :])
            both = jnp.concatenate([high, low], axis=0)
            part = lax.dot_general(both, split_rows[:, k * C : (k + 1) * C], NT, preferred_element_type=jnp.float32)
            total = part if total is None else total + part
        total = total.T
        held[:, r : r + RB] = (total[:R, :RB] + total[R:, RB:]) + (total[R:, :RB] + total[:R, RB:])
    x0, y0, zh0, core = place_ref[0], place_ref[1], place_ref[2], place_ref[4]
    for x in range(XS):
        for y in range(YS):
            for zh in range(2):
                dx = (x - x0 + XS) % XS
                dy = (y - y0 + YS) % YS
                slot = (zh ^ zh0) * 16 + jnp.where(core == 1, dy * 4 + dx, dx * 4 + dy)
                row = (x * YS + y) * 2 + zh
                out_ref[row : row + 1, 0:ROWS] = held[pl.ds(slot, 1), :]
    out_ref[:, ROWS : ROWS + OWN] = basis_ref[...]
    out_ref[:, ROWS + OWN :] = jnp.zeros_like(basis_ref)


def image_part(place, pieces, block, basis):
    return pl.pallas_call(
        image_kernel,
        in_specs=[SM] + [VM] * (len(pieces) + 2),
        out_specs=VM,
        out_shape=jax.ShapeDtypeStruct((R, ROWS + 2 * OWN), jnp.float32),
        scratch_shapes=[pltpu.VMEM((R, ROWS), jnp.float32), pltpu.VMEM((2 * R, K * C), jnp.bfloat16)],
        compiler_params=pltpu.CompilerParams(vmem_limit_bytes=8 << 20),
        name="image",
    )(place, *pieces, block, basis)


def in_order(second, mine, other):
    return jnp.concatenate([jnp.where(second, other, mine), jnp.where(second, mine, other)], axis=1)


def pair(second, mine, other):
    own = slice(ROWS, ROWS + OWN)
    image = mine[:, :ROWS] + other[:, :ROWS]
    return jnp.concatenate([image, in_order(second, mine[:, own], other[:, own])], axis=1)


def products_kernel(place_ref, *refs):
    parts, (image_ref, products_ref, held) = refs[:4], refs[4:]
    zh = place_ref[2]
    z = zh * 2 + place_ref[3]
    for step, part in enumerate(parts):
        held[pl.ds((z + step) % 4, 1)] = part[...][None]
    images = [held[2 * h, :, 0:ROWS] + held[2 * h + 1, :, 0:ROWS] for h in range(2)]
    image_ref[...] = jnp.where(zh == 0, images[0], images[1])
    image = jnp.concatenate(images, axis=1)
    basis = jnp.concatenate([held[i, :, ROWS:] for i in range(4)], axis=1)
    both = jnp.concatenate([image, basis], axis=0)
    total = lax.dot_general(both, both, NT, precision=HI, preferred_element_type=jnp.float32)
    products_ref[...] = jnp.concatenate([total[:R], total[R:]], axis=1)


def products(place, parts):
    return pl.pallas_call(
        products_kernel,
        in_specs=[SM] + [VM] * 4,
        out_specs=[VM] * 2,
        out_shape=[
            jax.ShapeDtypeStruct((R, ROWS), jnp.float32),
            jax.ShapeDtypeStruct((R, 4 * R), jnp.float32),
        ],
        scratch_shapes=[pltpu.VMEM((4, *parts[0].shape), jnp.float32)],
        compiler_params=pltpu.CompilerParams(vmem_limit_bytes=2 << 20),
        name="products",
    )(place, *parts)


def eliminate(work):
    lane = lax.broadcasted_iota(jnp.int32, (1, 4 * R), 1)
    done = []
    for k in range(0, R, 8):
        columns = [jnp.broadcast_to(work[:, k + m : k + m + 1], work.shape) for m in range(8)]
        rows = [work[k + m : k + m + 1, :] for m in range(8)]
        update = jnp.zeros_like(work)
        for m in range(8):
            at = k + m
            scale = lax.rsqrt(columns[m][at : at + 1, :])
            unit = rows[m] * scale
            column = columns[m] * scale
            done.append(jnp.where(lane >= at, unit, 0.0))
            for t in range(m + 1, 8):
                factor = columns[t][at : at + 1, :] * scale
                rows[t] = rows[t] - column[k + t : k + t + 1, :] * unit
                columns[t] = columns[t] - column * factor
            update = update + column * unit
        work = work - update
    return jnp.concatenate(done, axis=0)


def final_kernel(place_ref, products_ref, image_ref, basis_ref, new_ref, projection_ref, factor_ref):
    dot = functools.partial(lax.dot_general, precision=HI, preferred_element_type=jnp.float32)
    total = products_ref[0]
    for chip in range(1, XS * YS):
        total = total + products_ref[chip]
    squares = total[:, 0:R]
    first_t = total[:, R : 2 * R]
    first = total[:, 2 * R : 3 * R]
    basis_gram = total[:, 3 * R : 4 * R]
    projection = 2.0 * first - dot(basis_gram, first, NN)
    projection_t = 2.0 * first_t - dot(first_t, basis_gram, NN)
    projection_ref[...] = projection
    left = first - dot(basis_gram, projection, NN)
    gram = (squares - dot(first_t, projection, NN) - dot(projection_t, left, NN)) / N
    narrow = place_ref[3] * 2 + place_ref[4]
    own = image_ref[:, 0:64]
    for n in range(1, 4):
        own = jnp.where(narrow == n, image_ref[:, n * 64 : (n + 1) * 64], own)
    twice = own - dot(projection_t, basis_ref[...], NN)
    work = jnp.concatenate([gram, jnp.zeros((R, R), jnp.float32), twice], axis=1)
    rows = eliminate(work)
    factor_ref[...] = rows[:, 0:R].T
    new_ref[...] = rows[:, 2 * R : 4 * R]


def final(place, total, image, basis):
    return pl.pallas_call(
        final_kernel,
        in_specs=[SM] + [VM] * 3,
        out_specs=[VM] * 3,
        out_shape=[
            jax.ShapeDtypeStruct(basis.shape, jnp.float32),
            jax.ShapeDtypeStruct((R, R), jnp.float32),
            jax.ShapeDtypeStruct((R, R), jnp.float32),
        ],
        compiler_params=pltpu.CompilerParams(vmem_limit_bytes=2 << 20),
        name="final",
    )(place, total, image, basis)


def body(coefficients, tensor_blocks, basis_rows):
    coefficients = pltpu.with_memory_space_constraint(coefficients, pltpu.HBM)
    place = jnp.stack([lax.axis_index(axis) for axis in AXES]).astype(jnp.int32)

    own = tensor_blocks.reshape(K * LANES, C // LANES)
    held_own = hold(own)
    moved = [move(own, ring(step, 1)) for step in (1, 2, 3)]
    held_own, *moved = lax.optimization_barrier([held_own, *moved])
    row = jnp.stack([held_own, *moved])
    across = move(row, FROM_ZH)
    far, one, three = [move(row, ring(step, 0)) for step in (2, 1, 3)]
    far_across = move(far, FROM_ZH)
    coefficients, across = lax.optimization_barrier((coefficients, across))
    loaded = load(coefficients)
    one_across, three_across = [move(across, ring(step, 0)) for step in (1, 3)]
    pieces = [row, one, far, three, across, one_across, far_across, three_across]

    part = image_part(place, pieces, loaded, basis_rows)
    part = pair(place[4] == 1, part, move(part, FROM_CORE))
    image, total = products(place, [part] + [move(part, along_z(step)) for step in (1, 2, 3)])
    total = jnp.broadcast_to(total, (XS * YS, *total.shape))
    total = lax.all_to_all(total, ("x", "y"), 0, 0, tiled=True)
    return tuple(final(place, total, image, basis_rows))


def solution(mesh):
    mesh = Mesh(mesh.devices.reshape(XS, YS, 2, 2, 2), AXES)
    wide, narrow = AXES[:3], AXES[3:]
    in_specs = (P(None, wide, narrow), P(None, wide, narrow), P(None, AXES))
    out_specs = (P(None, AXES), P(), P())
    return jax.shard_map(body, mesh=mesh, in_specs=in_specs, out_specs=out_specs, check_vma=False)
```

```python
import functools

import jax
import jax.numpy as jnp
from jax import lax
from jax.experimental import pallas as pl
from jax.experimental.pallas import tpu as pltpu
from jax.sharding import Mesh, PartitionSpec as P

N = 8192
K = 8
R = 32
XS = 4
YS = 4
C = 2048
LANES = 16
ROWS = 256
RB = 128
OWN = 64
AXES = ("x", "y", "zh", "zl", "core")
HI = lax.Precision.HIGHEST
NT = (((1,), (1,)), ((), ()))
NN = (((1,), (0,)), ((), ()))
VM = pl.BlockSpec(memory_space=pltpu.VMEM)
SM = pl.BlockSpec(memory_space=pltpu.SMEM)


def flat(x, y, zh, zl, core):
    return ((x * YS + y) * 2 + zh) * 4 + zl * 2 + core


def sources(source_of):
    pairs = []
    for x in range(XS):
        for y in range(YS):
            for zh in range(2):
                for zl in range(2):
                    for core in range(2):
                        here = (x, y, zh, zl, core)
                        pairs.append((flat(*source_of(*here)), flat(*here)))
    return pairs


def ring(step, x_core):
    def source(x, y, zh, zl, core):
        if core == x_core:
            return (x + step) % XS, y, zh, zl, core
        return x, (y + step) % YS, zh, zl, core

    return sources(source)


FROM_ZH = sources(lambda x, y, zh, zl, core: (x, y, 1 - zh, zl, core))
FROM_CORE = sources(lambda x, y, zh, zl, core: (x, y, zh, zl, 1 - core))

def along_z(step):
    def source(x, y, zh, zl, core):
        z = (zh * 2 + zl + step) % 4
        return x, y, z // 2, z % 2, 1 - core

    return sources(source)


def move(value, pairs):
    return lax.ppermute(value, AXES, pairs)


def split(value):
    high = value.astype(jnp.bfloat16)
    low = (value - high.astype(jnp.float32)).astype(jnp.bfloat16)
    return high, low


def hold_kernel(source_ref, out_ref, sem):
    copy = pltpu.make_async_copy(source_ref, out_ref, sem)
    copy.start()
    copy.wait()


def hold(block):
    return pl.pallas_call(
        hold_kernel,
        in_specs=[pl.BlockSpec(memory_space=pltpu.HBM)],
        out_specs=VM,
        out_shape=jax.ShapeDtypeStruct(block.shape, jnp.float32),
        scratch_shapes=[pltpu.SemaphoreType.DMA],
        compiler_params=pltpu.CompilerParams(vmem_limit_bytes=1 << 20),
        name="hold",
    )(block)


def load_kernel(source_ref, out_ref, sem):
    copy = pltpu.make_async_copy(source_ref, out_ref, sem)
    copy.start()
    copy.wait()


def load(coefficients):
    return pl.pallas_call(
        load_kernel,
        in_specs=[pl.BlockSpec(memory_space=pltpu.HBM)],
        out_specs=VM,
        out_shape=pltpu.VMEM(coefficients.shape, jnp.float32),
        scratch_shapes=[pltpu.SemaphoreType.DMA],
        compiler_params=pltpu.CompilerParams(vmem_limit_bytes=1 << 20),
        name="load",
    )(coefficients)


def image_kernel(place_ref, *refs):
    pieces, (block, basis_ref, out_ref, held, split_rows) = refs[:8], refs[8:]
    for k in range(K):
        tiles = []
        for at in range(k * LANES, (k + 1) * LANES):
            tiles.append(jnp.concatenate([piece[:, at, :] for piece in pieces], axis=0))
        high, low = split(jnp.concatenate(tiles, axis=1))
        split_rows[0:R, k * C : (k + 1) * C] = high
        split_rows[R : 2 * R, k * C : (k + 1) * C] = low
    for r in range(0, ROWS, RB):
        total = None
        for k in range(K):
            high, low = split(block[k, r : r + RB, :])
            both = jnp.concatenate([high, low], axis=0)
            part = lax.dot_general(both, split_rows[:, k * C : (k + 1) * C], NT, preferred_element_type=jnp.float32)
            total = part if total is None else total + part
        total = total.T
        held[:, r : r + RB] = (total[:R, :RB] + total[R:, RB:]) + (total[R:, :RB] + total[:R, RB:])
    x0, y0, zh0, core = place_ref[0], place_ref[1], place_ref[2], place_ref[4]
    for x in range(XS):
        for y in range(YS):
            for zh in range(2):
                dx = (x - x0 + XS) % XS
                dy = (y - y0 + YS) % YS
                slot = (zh ^ zh0) * 16 + jnp.where(core == 1, dy * 4 + dx, dx * 4 + dy)
                row = (x * YS + y) * 2 + zh
                out_ref[row : row + 1, 0:ROWS] = held[pl.ds(slot, 1), :]
    out_ref[:, ROWS : ROWS + OWN] = basis_ref[...]
    out_ref[:, ROWS + OWN :] = jnp.zeros_like(basis_ref)


def image_part(place, pieces, block, basis):
    return pl.pallas_call(
        image_kernel,
        in_specs=[SM] + [VM] * (len(pieces) + 2),
        out_specs=VM,
        out_shape=jax.ShapeDtypeStruct((R, ROWS + 2 * OWN), jnp.float32),
        scratch_shapes=[pltpu.VMEM((R, ROWS), jnp.float32), pltpu.VMEM((2 * R, K * C), jnp.bfloat16)],
        compiler_params=pltpu.CompilerParams(vmem_limit_bytes=8 << 20),
        name="image",
    )(place, *pieces, block, basis)


def in_order(second, mine, other):
    return jnp.concatenate([jnp.where(second, other, mine), jnp.where(second, mine, other)], axis=1)


def pair(second, mine, other):
    own = slice(ROWS, ROWS + OWN)
    image = mine[:, :ROWS] + other[:, :ROWS]
    return jnp.concatenate([image, in_order(second, mine[:, own], other[:, own])], axis=1)


def products_kernel(place_ref, *refs):
    parts, (image_ref, products_ref, held) = refs[:4], refs[4:]
    zh = place_ref[2]
    z = zh * 2 + place_ref[3]
    for step, part in enumerate(parts):
        held[pl.ds((z + step) % 4, 1)] = part[...][None]
    images = [held[2 * h, :, 0:ROWS] + held[2 * h + 1, :, 0:ROWS] for h in range(2)]
    image_ref[...] = jnp.where(zh == 0, images[0], images[1])
    image = jnp.concatenate(images, axis=1)
    basis = jnp.concatenate([held[i, :, ROWS:] for i in range(4)], axis=1)
    both = jnp.concatenate([image, basis], axis=0)
    total = lax.dot_general(both, both, NT, precision=HI, preferred_element_type=jnp.float32)
    products_ref[...] = jnp.concatenate([total[:R], total[R:]], axis=1)


def products(place, parts):
    return pl.pallas_call(
        products_kernel,
        in_specs=[SM] + [VM] * 4,
        out_specs=[VM] * 2,
        out_shape=[
            jax.ShapeDtypeStruct((R, ROWS), jnp.float32),
            jax.ShapeDtypeStruct((R, 4 * R), jnp.float32),
        ],
        scratch_shapes=[pltpu.VMEM((4, *parts[0].shape), jnp.float32)],
        compiler_params=pltpu.CompilerParams(vmem_limit_bytes=2 << 20),
        name="products",
    )(place, *parts)


def eliminate(work):
    lane = lax.broadcasted_iota(jnp.int32, (1, 4 * R), 1)
    done = []
    for k in range(0, R, 16):
        columns = [jnp.broadcast_to(work[:, k + m : k + m + 1], work.shape) for m in range(16)]
        rows = [work[k + m : k + m + 1, :] for m in range(16)]
        update = jnp.zeros_like(work)
        for m in range(16):
            at = k + m
            scale = lax.rsqrt(columns[m][at : at + 1, :])
            unit = rows[m] * scale
            column = columns[m] * scale
            done.append(jnp.where(lane >= at, unit, 0.0))
            for t in range(m + 1, 16):
                factor = columns[t][at : at + 1, :] * scale
                rows[t] = rows[t] - column[k + t : k + t + 1, :] * unit
                columns[t] = columns[t] - column * factor
            update = update + column * unit
        work = work - update
    return jnp.concatenate(done, axis=0)


def final_kernel(place_ref, products_ref, image_ref, basis_ref, new_ref, projection_ref, factor_ref):
    dot = functools.partial(lax.dot_general, precision=HI, preferred_element_type=jnp.float32)
    total = products_ref[0]
    for chip in range(1, XS * YS):
        total = total + products_ref[chip]
    squares = total[:, 0:R]
    first_t = total[:, R : 2 * R]
    first = total[:, 2 * R : 3 * R]
    basis_gram = total[:, 3 * R : 4 * R]
    projection = 2.0 * first - dot(basis_gram, first, NN)
    projection_t = 2.0 * first_t - dot(first_t, basis_gram, NN)
    projection_ref[...] = projection
    left = first - dot(basis_gram, projection, NN)
    gram = (squares - dot(first_t, projection, NN) - dot(projection_t, left, NN)) / N
    narrow = place_ref[3] * 2 + place_ref[4]
    own = image_ref[:, 0:64]
    for n in range(1, 4):
        own = jnp.where(narrow == n, image_ref[:, n * 64 : (n + 1) * 64], own)
    twice = own - dot(projection_t, basis_ref[...], NN)
    work = jnp.concatenate([gram, jnp.zeros((R, R), jnp.float32), twice], axis=1)
    rows = eliminate(work)
    factor_ref[...] = rows[:, 0:R].T
    new_ref[...] = rows[:, 2 * R : 4 * R]


def final(place, total, image, basis):
    return pl.pallas_call(
        final_kernel,
        in_specs=[SM] + [VM] * 3,
        out_specs=[VM] * 3,
        out_shape=[
            jax.ShapeDtypeStruct(basis.shape, jnp.float32),
            jax.ShapeDtypeStruct((R, R), jnp.float32),
            jax.ShapeDtypeStruct((R, R), jnp.float32),
        ],
        compiler_params=pltpu.CompilerParams(vmem_limit_bytes=2 << 20),
        name="final",
    )(place, total, image, basis)


def body(coefficients, tensor_blocks, basis_rows):
    coefficients = pltpu.with_memory_space_constraint(coefficients, pltpu.HBM)
    place = jnp.stack([lax.axis_index(axis) for axis in AXES]).astype(jnp.int32)

    own = tensor_blocks.reshape(K * LANES, C // LANES)
    held_own = hold(own)
    moved = [move(own, ring(step, 1)) for step in (1, 2, 3)]
    held_own, *moved = lax.optimization_barrier([held_own, *moved])
    row = jnp.stack([held_own, *moved])
    across = move(row, FROM_ZH)
    far, one, three = [move(row, ring(step, 0)) for step in (2, 1, 3)]
    far_across = move(far, FROM_ZH)
    coefficients, across = lax.optimization_barrier((coefficients, across))
    loaded = load(coefficients)
    one_across, three_across = [move(across, ring(step, 0)) for step in (1, 3)]
    pieces = [row, one, far, three, across, one_across, far_across, three_across]

    part = image_part(place, pieces, loaded, basis_rows)
    part = pair(place[4] == 1, part, move(part, FROM_CORE))
    image, total = products(place, [part] + [move(part, along_z(step)) for step in (1, 2, 3)])
    total = jnp.broadcast_to(total, (XS * YS, *total.shape))
    total = lax.all_to_all(total, ("x", "y"), 0, 0, tiled=True)
    return tuple(final(place, total, image, basis_rows))


def solution(mesh):
    mesh = Mesh(mesh.devices.reshape(XS, YS, 2, 2, 2), AXES)
    wide, narrow = AXES[:3], AXES[3:]
    in_specs = (P(None, wide, narrow), P(None, wide, narrow), P(None, AXES))
    out_specs = (P(None, AXES), P(), P())
    return jax.shard_map(body, mesh=mesh, in_specs=in_specs, out_specs=out_specs, check_vma=False)
```
